512 devices in a mesh: dp: 32 (over y_lo, z), fsdp: 16 (over x, y_hi, core).
Axes of the slice: x: 4, y: 8 (y_hi: 2, y_lo: 4; y = y_hi * 4 + y_lo), z: 8, core: 2. Of those that a mesh axis runs over, the one named last changes fastest.
Arguments:
- tokens: bfloat16 [65536, 2048], P(('dp', 'fsdp')), may hold values from -6 to 6
- upstream: bfloat16 [65536, 512], P(('dp', 'fsdp')), may hold values from -6 to 6
- value_weight: bfloat16 [2048, 512], P('fsdp'), may hold values from -0.125 to 0.125
- forget_label: int32 [32], P('dp'), may hold values 0 or 1
- copy_index: int32 [32], P('dp'), may hold values from 0 to 1, as said below
- adv_rate: float32 [2], replicated, may hold values from 0.5 to 2
Outputs:
- meta_grad: float32 [2048, 512], P('fsdp')
The draws below stay inside these ranges and needn't reach their ends.
Inputs may be any that keep to these rules, and one draw needn't show every extreme that they name: `copy_index`: each of the 2 copies is named by exactly 16 sequences.
All inputs are finite; a program needn't handle non-finite values. No bound on the sum of `forget_label` on one device may be relied on, other than what follows from the above.
Results may differ from the reference program's by a relative error of at most 0.0056.
Values may be sent and summed in bfloat16 or wider, within the bound.
A program may use at most 64 MiB of HBM per device.

```python
import math
import jax
import jax.numpy as jnp

DW = 2048
E = 512
COPIES = 2
LEN = 2048
SEQS = 32
TOKENS = 65536


def draw_copy_index(key, part):
    order = jax.random.permutation(key, SEQS)
    return (order % COPIES).astype(jnp.int32)


def set_ends(entries, key, least, largest):
    longest = entries.shape.index(max(entries.shape))
    spots = []
    for shift in (0, 1):
        where = [jax.random.randint(jax.random.fold_in(key, axis), (), 0, length) for axis, length in enumerate(entries.shape)]
        where[longest] = (where[longest] + shift) % entries.shape[longest]
        spots.append(tuple(where))
    return entries.at[spots[0]].set(least).at[spots[1]].set(largest)


def shard_levels(own_key, dims, shards, least, high):
    gain = 1.0
    for position, parts in shards:
        draws = jax.random.uniform(jax.random.fold_in(jax.random.fold_in(own_key, 6), position), (parts,), jnp.float32, least / len(shards), high / len(shards))
        gain = gain * jnp.repeat(jnp.exp(draws), dims[position] // parts).reshape((-1,) + (1,) * (len(dims) - 1 - position))
    return gain


def bell_draw(key, shape, scale, bound, split=(), held_as=jnp.bfloat16):
    values = scale * jax.random.normal(key, shape, jnp.float32)
    if split:
        values = values * shard_levels(key, shape, split, -0.22, 0.18)
    return jnp.clip(values, -bound, bound).astype(held_as)


def setup_inputs(seed: int = 0) -> dict:
    keys = jax.random.split(jax.random.key(seed), 7)
    tokens = bell_draw(keys[0], (TOKENS, DW), 1.0, 6.0, ((0, 512),))
    upstream = bell_draw(keys[1], (TOKENS, E), 1.0, 6.0, ((0, 512),))
    value_weight = bell_draw(keys[2], (DW, E), DW ** -0.5, 0.125, ((0, 16),))
    forget_label = set_ends((jax.random.randint(keys[3], (SEQS,), 0, 2) < 1).astype(jnp.int32), jax.random.fold_in(keys[3], 1), 0, 1)
    copy_index = draw_copy_index(jax.random.fold_in(keys[6], 71), 0)
    adv_rate = jnp.clip(jnp.exp(jax.random.uniform(keys[5], (COPIES,), jnp.float32, math.log(0.5), math.log(2.0))), 0.5, 2.0)
    return dict(tokens=tokens, upstream=upstream, value_weight=value_weight, forget_label=forget_label, copy_index=copy_index, adv_rate=adv_rate)


def first_slope(value):
    sig = jax.nn.sigmoid(value)
    return sig * (1.0 + value * (1.0 - sig))


def second_slope(value):
    sig = jax.nn.sigmoid(value)
    return sig * (1.0 - sig) * (2.0 + value * (1.0 - 2.0 * sig))


def reference(tokens, upstream, value_weight, forget_label, copy_index, adv_rate):
    inputs = tokens.reshape(SEQS, LEN, DW).astype(jnp.float32)
    upward = upstream.reshape(SEQS, LEN, E).astype(jnp.float32)
    forget = forget_label.astype(jnp.float32)[:, None, None]
    onehot = (copy_index[:, None] == jnp.arange(COPIES, dtype=jnp.int32)[None, :]).astype(jnp.float32)
    weight_f = value_weight.astype(jnp.float32)
    primal = jnp.einsum("std,de->ste", inputs, weight_f)
    delta_adv = (forget * upward * first_slope(primal) / LEN).astype(jnp.bfloat16)
    per_seq = jnp.einsum("std,ste->sde", inputs, delta_adv.astype(jnp.float32))
    grad_copy = jnp.einsum("sc,sde->cde", onehot, per_seq)
    attacked = (weight_f[None] - adv_rate[:, None, None] * grad_copy).astype(jnp.bfloat16)
    attacked_seq = jnp.einsum("sc,cde->sde", onehot, attacked.astype(jnp.float32))
    altered = jnp.einsum("std,sde->ste", inputs, attacked_seq)
    delta_out = ((1.0 - 2.0 * forget) * upward * first_slope(altered) / LEN).astype(jnp.bfloat16)
    outer_seq = jnp.einsum("std,ste->sde", inputs, delta_out.astype(jnp.float32))
    outer_copy = jnp.einsum("sc,sde->cde", onehot, outer_seq)
    tangent = outer_copy.astype(jnp.bfloat16)
    tangent_seq = jnp.einsum("sc,cde->sde", onehot, tangent.astype(jnp.float32))
    forward_tangent = jnp.einsum("std,sde->ste", inputs, tangent_seq)
    delta_curv = (forget * upward * second_slope(primal) * forward_tangent / LEN).astype(jnp.bfloat16)
    curv_seq = jnp.einsum("std,ste->sde", inputs, delta_curv.astype(jnp.float32))
    rate_seq = jnp.sum(onehot * adv_rate[None, :], axis=1)
    curv_sum = jnp.einsum("s,sde->de", rate_seq, curv_seq)
    scale = (float(LEN) / float(SEQS)) ** 0.5
    return scale * (jnp.sum(outer_copy, axis=0) - curv_sum)
```

```python
import jax
import jax.numpy as jnp
from jax import lax
from jax.experimental import pallas as pl
from jax.experimental.pallas import tpu as pltpu
from jax.sharding import PartitionSpec as P

F32, BF16 = jnp.float32, jnp.bfloat16
NX, NYL, N = 4, 4, 8
TOK, DW, E, B, CH = 128, 2048, 512, 64, 128
LEN = 2048.0
SCALE = 8.0


def first_slope(value):
    sig = jax.nn.sigmoid(value)
    return sig * (1.0 + value * (1.0 - sig))


def second_slope(value):
    sig = jax.nn.sigmoid(value)
    return sig * (1.0 - sig) * (2.0 + value * (1.0 - 2.0 * sig))


W_, R_, C_ = 0, 1, 2


def rs1_(s, k):
    return 4 + 2 * s + k


def rs2_(s, k):
    return 10 + 2 * s + k


def ag2_(s, k):
    return 16 + 2 * s + k


def ag1_(s, k):
    return 20 + 2 * s + k


F1_, F2_, F3_, X_, GROUPS = 24, 26, 28, 29, 46


def chunk_of(k, p):
    return (p % 4) * 4 + (p // 4) * 2 + k


def kernel(
    tok_ref, up_ref, w_ref, forget_ref, copy_ref, rate_ref, out_ref,
    xbuf, wsrc, wrecv, rsrc, rrecv, crecv, wt, wown, prim, curv, delta,
    s1, r1, s2, r2, s2c, r2c, a2s, a2r, a1s, a1r, osum, tile, f1r, f2r, f3r,
    ssem, rsem, lsem,
):
    dp, fs = lax.axis_index("dp"), lax.axis_index("fsdp")
    yl, z = dp // 8, dp % 8
    x, yh, c = fs // 4, (fs // 2) % 2, fs % 2
    y = yh * 4 + yl
    place = (y, z)

    def ring_device(ring, p):
        if ring == 0:
            return ((p % 4) * 8 + z, x * 4 + (p // 4) * 2 + c)
        return (yl * 8 + p, fs)

    def group_device(dx, dc):
        return (dp, ((x + dx) % NX) * 4 + yh * 2 + (c + dc) % 2)

    def mirror_device(dx, dc):
        return ((3 - yl) * 8 + z, ((x + dx) % NX) * 4 + (1 - yh) * 2 + (c + dc) % 2)

    def send(src, dst, out_group, in_group, device):
        pltpu.make_async_remote_copy(
            src_ref=src, dst_ref=dst, send_sem=ssem.at[out_group], recv_sem=rsem.at[in_group],
            device_id=device, device_id_type=pl.DeviceIdType.MESH,
        ).start()

    def arrived(ref, group):
        pltpu.make_async_copy(ref, ref, rsem.at[group]).wait()

    def gone(ref, group):
        pltpu.make_async_copy(ref, ref, ssem.at[group]).wait()

    def spread(ring, group, source, dst):
        me = place[ring]

        def step(o, carry):
            p = (me + o) % N
            send(source(p), dst.at[me], group, group, ring_device(ring, p))
            return carry

        lax.fori_loop(1, N, step, 0)

    own = pltpu.make_async_copy(tok_ref, xbuf.at[pl.ds(0, TOK)], lsem)
    own.start()
    barrier = pltpu.get_barrier_semaphore()
    for dx in range(NX):
        for dc in range(2):
            if dx or dc:
                pl.semaphore_signal(barrier, inc=1, device_id=group_device(dx, dc), device_id_type=pl.DeviceIdType.MESH)
            pl.semaphore_signal(barrier, inc=1, device_id=mirror_device(dx, dc), device_id_type=pl.DeviceIdType.MESH)
    for ring in range(2):

        def greet(o, carry, ring=ring):
            device = ring_device(ring, (place[ring] + o) % N)
            pl.semaphore_signal(barrier, inc=1, device_id=device, device_id_type=pl.DeviceIdType.MESH)
            return carry

        lax.fori_loop(1, N, greet, 0)

    wsrc[...] = w_ref[...].T.reshape(8, B, CH)
    rsrc[...] = up_ref[...].T.reshape(8, B, TOK)
    copy = copy_ref[0].astype(F32)
    forget = forget_ref[0].astype(F32)
    rate0, rate1 = rate_ref[0], rate_ref[1]
    own_rate = rate0 * (1.0 - copy) + rate1 * copy
    crecv[0, y] = jnp.full((8, 128), copy, F32)
    crecv[1, z] = jnp.full((8, 128), copy, F32)
    own.wait()
    pl.semaphore_wait(barrier, 29)

    block = 2 * x + c
    for dx in range(NX):
        for dc in range(2):
            to = 2 * ((x + dx) % NX) + (c + dc) % 2
            if dx or dc:
                send(wsrc.at[to], wrecv.at[fs], W_, W_, group_device(dx, dc))
            send(wsrc.at[to], wrecv.at[fs], W_, W_, mirror_device(dx, dc))
    wrecv[fs] = wsrc[block]
    for dx in range(NX):
        for dc in range(2):
            if dx or dc:
                to = 2 * ((x + dx) % NX) + (c + dc) % 2
                send(rsrc.at[to], rrecv.at[2 * (-dx % NX) + dc], R_, R_, group_device(dx, dc))
    rrecv[0] = rsrc[block]

    def part(slot, half):
        return xbuf.at[pl.ds(slot * TOK + half * (TOK // 2), TOK // 2)]

    def send_part(from_slot, to_slot, half, dx, dc):
        send(part(from_slot, half), part(to_slot, half), X_, X_ + 1 + 2 * to_slot + half, group_device(dx, dc))

    def part_arrived(slot, half):
        arrived(part(slot, half), X_ + 1 + 2 * slot + half)

    send_part(0, 6, 0, 1, 0)
    send_part(0, 2, 1, 3, 0)
    send_part(0, 6, 1, 1, 0)
    send_part(0, 2, 0, 3, 0)
    send_part(0, 1, 0, 0, 1)
    send_part(0, 1, 1, 0, 1)
    for ring in range(2):
        spread(ring, C_ + ring, lambda p, ring=ring: crecv.at[ring, place[ring]], crecv.at[ring])

    arrived(wrecv.at[pl.ds(0, 15)], W_)
    for f in range(16):
        wt[:, f * CH:(f + 1) * CH] = wrecv[f]
    for k in range(2):
        wown[k] = wrecv[chunk_of(k, place[k])].astype(F32).reshape(8, 8, CH)
    arrived(rrecv.at[pl.ds(0, 7)], R_)

    def first_pass(slot):
        rows = slice(slot * TOK, (slot + 1) * TOK)
        value = lax.dot_general(wt[...], xbuf[rows, :], (((1,), (1,)), ((), ())), preferred_element_type=F32)
        prim[:, rows] = value
        delta[:, rows] = (forget * rrecv[slot].astype(F32) * first_slope(value) / LEN).astype(BF16)

    first_pass(0)
    part_arrived(6, 0)
    send_part(6, 4, 0, 1, 0)
    send_part(6, 7, 0, 0, 1)
    part_arrived(2, 1)
    send_part(2, 4, 1, 3, 0)
    send_part(2, 3, 1, 0, 1)
    part_arrived(1, 0)
    part_arrived(1, 1)
    first_pass(1)
    part_arrived(6, 1)
    send_part(6, 7, 1, 0, 1)
    part_arrived(2, 0)
    send_part(2, 3, 0, 0, 1)
    first_pass(6)
    first_pass(2)
    for slot in (7, 3):
        part_arrived(slot, 0)
        part_arrived(slot, 1)
        first_pass(slot)
    for half in range(2):
        part_arrived(4, half)
        send_part(4, 5, half, 0, 1)
    first_pass(4)
    part_arrived(5, 0)
    part_arrived(5, 1)
    first_pass(5)

    def reduce_first(s, factor=None):
        left = delta[...]

        def start(o):
            for k in range(2):
                p = (place[k] + o) % N
                send(s1.at[s, k, p], r1.at[s, k, place[k]], rs1_(s, k), rs1_(s, k), ring_device(k, p))

        def step(i, carry):
            o = i + 1
            spots = [(place[k] + o) % N for k in range(2)]
            right = jnp.concatenate(
                [xbuf[:, pl.ds(pl.multiple_of(chunk_of(k, spots[k]) * CH, CH), CH)] for k in range(2)], axis=1)
            sums = jnp.dot(left, right, preferred_element_type=F32)
            if factor is not None:
                sums = factor * sums
            for k in range(2):
                s1[s, k, spots[k]] = sums[:, k * CH:(k + 1) * CH].astype(BF16)
            pl.when(i > 0)(lambda: start(i))
            return carry

        lax.fori_loop(0, N, step, 0)

    def own_first(s, k):
        r1[s, k, place[k]] = s1[s, k, place[k]]

    def reduce_second(s, k):
        arrived(r1.at[s, k, pl.ds(0, 7)], rs1_(s, k))
        own_first(s, k)
        ring = 1 - k
        sums = [jnp.zeros((B, CH), F32) for _ in range(2)]
        for p in range(N):
            piece = r1[s, k, p].astype(F32)
            mark = crecv[k, p, 0:1, :]
            sums[0] = sums[0] + piece * (1.0 - mark)
            sums[1] = sums[1] + piece * mark
        for copy_at in range(2):
            s2[s, k, :, copy_at] = sums[copy_at].reshape(8, 8, CH)
        spread(ring, rs2_(s, k), lambda p: s2.at[s, k, p], r2.at[s, k])

    def owned(s, k):
        me = place[1 - k]
        r2[s, k, me] = s2[s, k, me]
        arrived(r2.at[s, k, pl.ds(0, 7)], rs2_(s, k))
        total = r2[s, k, 0]
        for p in range(1, N):
            total = total + r2[s, k, p]
        return total[0], total[1]

    def gather_second(s, k, piece0, piece1):
        ring = 1 - k
        a2s[s, k] = jnp.concatenate([piece0, piece1], axis=0).astype(BF16)
        spread(ring, ag2_(s, k), lambda p: a2s.at[s, k], a2r.at[s, k])

    def gather_first(s, k):
        a2r[s, k, place[1 - k]] = a2s[s, k]
        arrived(a2r.at[s, k, pl.ds(0, 7)], ag2_(s, k))
        both = a2r[s, k].astype(F32)
        zero, one = both[:, :8].reshape(B, CH), both[:, 8:].reshape(B, CH)
        for p in range(N):
            mark = crecv[k, p, 0:1, :]
            a1s[s, k, p] = (zero * (1.0 - mark) + one * mark).astype(BF16)
        spread(k, ag1_(s, k), lambda p: a1s.at[s, k, p], a1r.at[s, k])

    def gathered(s):
        for k in range(2):
            a1r[s, k, place[k]] = a1s[s, k, place[k]]
            arrived(a1r.at[s, k, pl.ds(0, 7)], ag1_(s, k))
            for p in range(N):
                f = chunk_of(k, p)
                wt[:, f * CH:(f + 1) * CH] = a1r[s, k, p]

    def project(quarter):
        rows = slice(quarter * 256, (quarter + 1) * 256)
        return rows, lax.dot_general(wt[...], xbuf[rows, :], (((1,), (1,)), ((), ())), preferred_element_type=F32)

    def upward(rows):
        first = rows.start // TOK
        return jnp.concatenate([rrecv[first].astype(F32), rrecv[first + 1].astype(F32)], axis=1)

    reduce_first(0)
    for k in range(2):
        arrived(crecv.at[k, pl.ds(0, 7)], C_ + k)
    for quarter in range(4):
        rows = slice(quarter * 256, (quarter + 1) * 256)
        curv[:, rows] = forget * upward(rows) * second_slope(prim[:, rows])
    for k in range(2):
        reduce_second(0, k)
    for k in range(2):
        grad0, grad1 = owned(0, k)
        base = wown[k, place[1 - k]]
        gather_second(0, k, base - rate0 * grad0, base - rate1 * grad1)
    for k in range(2):
        gather_first(0, k)
    gathered(0)

    for quarter in range(4):
        rows, value = project(quarter)
        delta[:, rows] = ((1.0 - 2.0 * forget) * upward(rows) * first_slope(value) / LEN).astype(BF16)
    reduce_first(1)
    for k in range(2):
        reduce_second(1, k)
    for k in range(2):
        outer0, outer1 = owned(1, k)
        osum[k] = outer0 + outer1
        gather_second(1, k, outer0, outer1)
    for k in range(2):
        gather_first(1, k)
    gathered(1)

    for quarter in range(4):
        rows, value = project(quarter)
        delta[:, rows] = (curv[:, rows] * value / LEN).astype(BF16)
    reduce_first(2, own_rate)
    for k in range(2):
        arrived(r1.at[2, k, pl.ds(0, 7)], rs1_(2, k))
        own_first(2, k)
        total = r1[2, k, 0].astype(F32)
        for p in range(1, N):
            total = total + r1[2, k, p].astype(F32)
        s2c[k] = total.reshape(8, 8, CH)
        spread(1 - k, rs2_(2, k), lambda p: s2c.at[k, p], r2c.at[k])
    for k in range(2):
        me = place[1 - k]
        r2c[k, me] = s2c[k, me]
        arrived(r2c.at[k, pl.ds(0, 7)], rs2_(2, k))
        total = r2c[k, 0]
        for p in range(1, N):
            total = total + r2c[k, p]
        tile[k] = SCALE * (osum[k] - total)

    spots = (yl, z % 4)
    targets = [spots[k] * 4 + yh * 2 + k for k in range(2)]
    for k in range(2):

        @pl.when(fs != targets[k])
        def _(k=k):
            send(tile.at[k], f1r.at[block], F1_ + k, F1_, (dp, targets[k]))

        @pl.when(fs == targets[k])
        def _(k=k):
            f1r[block] = tile[k]

    @pl.when(c == 0)
    def _():
        @pl.when(x == yl)
        def _():
            arrived(f1r.at[pl.ds(0, 7)], F1_)
            for o in range(1, NYL):
                send(f1r, f2r.at[0], F2_, F2_, (((yl + o) % NYL) * 8 + z, fs))
            f2r[0] = f1r[...]
            gone(f3r.at[pl.ds(0, 3)], F2_)

        @pl.when(x != yl)
        def _():
            arrived(f2r.at[0], F2_)

        def step(o, carry):
            p = (z + o) % N
            send(f2r.at[0], f3r.at[z], F3_, F3_, ring_device(1, p))
            return carry

        lax.fori_loop(1, N, step, 0)
        f3r[z] = f2r[0]

    @pl.when(c == 1)
    def _():
        @pl.when(x == z % 4)
        def _():
            arrived(f1r.at[pl.ds(0, 7)], F1_)

            def step(o, carry):
                p = (z + o) % N
                send(f1r, f2r.at[z // 4], F2_, F2_ + z // 4, ring_device(1, p))
                return carry

            lax.fori_loop(1, N, step, 0)
            f2r[z // 4] = f1r[...]
            arrived(f2r.at[1 - z // 4], F2_ + 1 - z // 4)
            gone(f3r.at[pl.ds(0, 7)], F2_)

        @pl.when(x != z % 4)
        def _():
            arrived(f2r.at[0], F2_)
            arrived(f2r.at[1], F2_ + 1)

        def step(o, carry):
            p = (y + o) % N
            send(f2r.at[p // 4], f3r.at[y], F3_, F3_, ring_device(0, p))
            return carry

        lax.fori_loop(1, N, step, 0)
        f3r[y] = f2r[yh]

    arrived(f3r.at[pl.ds(0, 7)], F3_)
    for pair in range(4):
        both = jnp.concatenate([f3r[:, 2 * pair + i].reshape(B, CH) for i in range(2)], axis=0)
        out_ref[:, pair * 128:(pair + 1) * 128] = both.T

    gone(wrecv.at[pl.ds(0, 15)], W_)
    gone(rrecv.at[pl.ds(0, 7)], R_)
    gone(xbuf.at[pl.ds(0, 14 * (TOK // 2))], X_)
    for k in range(2):
        gone(crecv.at[k, pl.ds(0, 7)], C_ + k)
        for s in range(3):
            gone(r1.at[s, k, pl.ds(0, 7)], rs1_(s, k))
        for s in range(2):
            gone(r2.at[s, k, pl.ds(0, 7)], rs2_(s, k))
            gone(a2r.at[s, k, pl.ds(0, 7)], ag2_(s, k))
            gone(a1r.at[s, k, pl.ds(0, 7)], ag1_(s, k))
        gone(r2c.at[k, pl.ds(0, 7)], rs2_(2, k))

        @pl.when(fs != targets[k])
        def _(k=k):
            gone(tile.at[k], F1_ + k)

    gone(f3r.at[pl.ds(0, 7)], F3_)


def local(tokens, upstream, value_weight, forget_label, copy_index, adv_rate):
    vmem, smem = pl.BlockSpec(memory_space=pltpu.VMEM), pl.BlockSpec(memory_space=pltpu.SMEM)
    return pl.pallas_call(
        kernel,
        out_shape=jax.ShapeDtypeStruct((CH, E), F32),
        in_specs=[pl.BlockSpec(memory_space=pl.ANY), vmem, vmem, smem, smem, smem],
        out_specs=vmem,
        scratch_shapes=[
            pltpu.VMEM((8 * TOK, DW), BF16),
            pltpu.VMEM((8, B, CH), BF16),
            pltpu.VMEM((16, B, CH), BF16),
            pltpu.VMEM((8, B, TOK), BF16),
            pltpu.VMEM((8, B, TOK), BF16),
            pltpu.VMEM((2, 8, 8, 128), F32),
            pltpu.VMEM((B, DW), BF16),
            pltpu.VMEM((2, 8, 8, CH), F32),
            pltpu.VMEM((B, 8 * TOK), F32),
            pltpu.VMEM((B, 8 * TOK), F32),
            pltpu.VMEM((B, 8 * TOK), BF16),
            pltpu.VMEM((3, 2, 8, B, CH), BF16),
            pltpu.VMEM((3, 2, 8, B, CH), BF16),
            pltpu.VMEM((2, 2, 8, 2, 8, CH), F32),
            pltpu.VMEM((2, 2, 8, 2, 8, CH), F32),
            pltpu.VMEM((2, 8, 8, CH), F32),
            pltpu.VMEM((2, 8, 8, CH), F32),
            pltpu.VMEM((2, 2, 16, CH), BF16),
            pltpu.VMEM((2, 2, 8, 16, CH), BF16),
            pltpu.VMEM((2, 2, 8, B, CH), BF16),
            pltpu.VMEM((2, 2, 8, B, CH), BF16),
            pltpu.VMEM((2, 8, CH), F32),
            pltpu.VMEM((2, 8, CH), F32),
            pltpu.VMEM((8, 8, CH), F32),
            pltpu.VMEM((2, 8, 8, CH), F32),
            pltpu.VMEM((8, 8, 8, CH), F32),
            pltpu.SemaphoreType.DMA((GROUPS,)),
            pltpu.SemaphoreType.DMA((GROUPS,)),
            pltpu.SemaphoreType.DMA,
        ],
        compiler_params=pltpu.CompilerParams(collective_id=0, has_side_effects=True, vmem_limit_bytes=48 << 20),
        name="meta_grad",
    )(tokens, upstream, value_weight, forget_label, copy_index, adv_rate)


def solution(mesh):
    in_specs = (
        P(("dp", "fsdp"), None),
        P(("dp", "fsdp"), None),
        P("fsdp", None),
        P("dp"),
        P("dp"),
        P(),
    )
    return jax.shard_map(local, mesh=mesh, in_specs=in_specs, out_specs=P("fsdp", None), check_vma=False)
```

```python
import jax
import jax.numpy as jnp
from jax import lax
from jax.experimental import pallas as pl
from jax.experimental.pallas import tpu as pltpu
from jax.sharding import PartitionSpec as P

F32, BF16 = jnp.float32, jnp.bfloat16
NX, NYL, N = 4, 4, 8
TOK, DW, E, B, CH = 128, 2048, 512, 64, 128
LEN = 2048.0
SCALE = 8.0


def first_slope(value):
    sig = jax.nn.sigmoid(value)
    return sig * (1.0 + value * (1.0 - sig))


def second_slope(value):
    sig = jax.nn.sigmoid(value)
    return sig * (1.0 - sig) * (2.0 + value * (1.0 - 2.0 * sig))


QR = TOK // 4
W_, R_, C_ = 0, 1, 2


def rs1_(s, k):
    return 4 + 2 * s + k


def rs2_(s, k):
    return 10 + 2 * s + k


def ag2_(s, k):
    return 16 + 2 * s + k


def ag1_(s, k):
    return 20 + 2 * s + k


F1_, F2_, F3_, WY_, X_, GROUPS = 24, 26, 28, 29, 30, 63


def far_first(i):
    return 4 + (2 * (i % 2) - 1) * ((i + 1) // 2)


def chunk_of(k, p):
    return (p % 4) * 4 + (p // 4) * 2 + k


def kernel(
    tok_ref, up_ref, w_ref, forget_ref, copy_ref, rate_ref, out_ref,
    xbuf, wbuf, ubuf, wsrc, wx, wy, rsrc, rrecv, crecv, wt, wown, prim, curv, delta,
    s1, r1, s2, r2, s2c, r2c, a2s, a2r, a1s, a1r, osum, tile, f1r, f2s, f2r, f3r,
    ssem, rsem, lsem,
):
    dp, fs = lax.axis_index("dp"), lax.axis_index("fsdp")
    yl, z = dp // 8, dp % 8
    x, yh, c = fs // 4, (fs // 2) % 2, fs % 2
    y = yh * 4 + yl
    place = (y, z)

    def ring_device(ring, p):
        if ring == 0:
            return ((p % 4) * 8 + z, x * 4 + (p // 4) * 2 + c)
        return (yl * 8 + p, fs)

    def group_device(dx, dc):
        return (dp, ((x + dx) % NX) * 4 + yh * 2 + (c + dc) % 2)

    def send(src, dst, out_group, in_group, device):
        pltpu.make_async_remote_copy(
            src_ref=src, dst_ref=dst, send_sem=ssem.at[out_group], recv_sem=rsem.at[in_group],
            device_id=device, device_id_type=pl.DeviceIdType.MESH,
        ).start()

    def arrived(ref, group):
        pltpu.make_async_copy(ref, ref, rsem.at[group]).wait()

    def gone(ref, group):
        pltpu.make_async_copy(ref, ref, ssem.at[group]).wait()

    def spread(ring, group, source, dst):
        me = place[ring]

        def step(i, carry):
            p = (me + far_first(i)) % N
            send(source(p), dst.at[me], group, group, ring_device(ring, p))
            return carry

        lax.fori_loop(0, N - 1, step, 0)

    own = [
        pltpu.make_async_copy(src, dst, lsem.at[i])
        for i, (src, dst) in enumerate(((w_ref, wbuf), (up_ref, ubuf), (tok_ref, xbuf.at[pl.ds(0, TOK)])))
    ]
    for copy_in in own:
        copy_in.start()
    barrier = pltpu.get_barrier_semaphore()
    for dx in range(NX):
        for dc in range(2):
            if dx or dc:
                pl.semaphore_signal(barrier, inc=1, device_id=group_device(dx, dc), device_id_type=pl.DeviceIdType.MESH)
    for ring in range(2):

        def greet(o, carry, ring=ring):
            device = ring_device(ring, (place[ring] + o) % N)
            pl.semaphore_signal(barrier, inc=1, device_id=device, device_id_type=pl.DeviceIdType.MESH)
            return carry

        lax.fori_loop(1, N, greet, 0)

    own[0].wait()
    wsrc[...] = wbuf[...].T.reshape(8, 4, 16, CH)
    own[1].wait()
    rsrc[...] = ubuf[...].T.reshape(8, B, TOK)
    copy = copy_ref[0].astype(F32)
    forget = forget_ref[0].astype(F32)
    rate0, rate1 = rate_ref[0], rate_ref[1]
    own_rate = rate0 * (1.0 - copy) + rate1 * copy
    crecv[0, y] = jnp.full((8, 128), copy, F32)
    crecv[1, z] = jnp.full((8, 128), copy, F32)
    own[2].wait()
    pl.semaphore_wait(barrier, 21)

    block = 2 * x + c
    others = [(dx, dc) for dx in range(NX) for dc in range(2) if dx or dc]
    for dx, dc in others:
        to = 2 * ((x + dx) % NX) + (c + dc) % 2
        send(wsrc.at[to, yl], wx.at[block], W_, W_, group_device(dx, dc))

    def part(slot, quarter):
        return xbuf.at[pl.ds(slot * TOK + quarter * QR, QR)]

    def send_part(from_slot, to_slot, quarter, dx, dc):
        group = X_ + 1 + 4 * to_slot + quarter
        send(part(from_slot, quarter), part(to_slot, quarter), X_, group, group_device(dx, dc))

    def part_arrived(slot, quarter):
        arrived(part(slot, quarter), X_ + 1 + 4 * slot + quarter)

    for i in range(4):
        send_part(0, 6, i, 1, 0)
        send_part(0, 2, 3 - i, 3, 0)
        send_part(0, 1, i, 0, 1)
    for dx, dc in others:
        to = 2 * ((x + dx) % NX) + (c + dc) % 2
        send(rsrc.at[to], rrecv.at[2 * (-dx % NX) + dc], R_, R_, group_device(dx, dc))
    rrecv[0] = rsrc[block]
    for ring in range(2):
        spread(ring, C_ + ring, lambda p, ring=ring: crecv.at[ring, place[ring]], crecv.at[ring])

    wx[block] = wsrc[block, yl]
    arrived(wx.at[pl.ds(0, 7)], W_)
    spread(0, WY_, lambda p: wx, wy)
    wy[y] = wx[...]

    def first_pass(slot):
        rows = slice(slot * TOK, (slot + 1) * TOK)
        value = lax.dot_general(wt[...], xbuf[rows, :], (((1,), (1,)), ((), ())), preferred_element_type=F32)
        prim[:, rows] = value
        delta[:, rows] = (forget * rrecv[slot].astype(F32) * first_slope(value) / LEN).astype(BF16)

    def pass_on(slot, quarter):
        part_arrived(slot, quarter)
        send_part(slot, slot + 1, quarter, 0, 1)

    for i in range(2):
        part_arrived(6, i)
        send_part(6, 4, i, 1, 0)
        send_part(6, 7, i, 0, 1)
        part_arrived(2, 3 - i)
        send_part(2, 4, 3 - i, 3, 0)
        send_part(2, 3, 3 - i, 0, 1)
    for i in range(2):
        pass_on(6, 2 + i)
        pass_on(2, 1 - i)
    arrived(wy.at[pl.ds(0, 7)], WY_)
    for p in range(N):
        for b in range(8):
            f = (b // 2) * 4 + (p // 4) * 2 + b % 2
            wt[(p % 4) * 16:(p % 4) * 16 + 16, f * CH:(f + 1) * CH] = wy[p, b]
    for k in range(2):
        first = pl.multiple_of(chunk_of(k, place[k]) * CH, CH)
        wown[k] = wt[:, pl.ds(first, CH)].astype(F32).reshape(8, 8, CH)
    for i in range(4):
        part_arrived(1, i)
    arrived(rrecv.at[pl.ds(0, 7)], R_)
    first_pass(0)
    first_pass(1)
    pass_on(4, 0)
    pass_on(4, 3)
    first_pass(6)
    first_pass(2)
    for slot in (7, 3):
        for i in range(4):
            part_arrived(slot, i)
        first_pass(slot)
    pass_on(4, 1)
    pass_on(4, 2)
    first_pass(4)
    for i in range(4):
        part_arrived(5, i)
    first_pass(5)

    def reduce_first(s, factor=None):
        left = delta[...]

        def start(i):
            for k in range(2):
                p = (place[k] + far_first(i)) % N
                send(s1.at[s, k, p], r1.at[s, k, place[k]], rs1_(s, k), rs1_(s, k), ring_device(k, p))

        def step(i, carry):
            spots = [(place[k] + far_first(i)) % N for k in range(2)]
            right = jnp.concatenate(
                [xbuf[:, pl.ds(pl.multiple_of(chunk_of(k, spots[k]) * CH, CH), CH)] for k in range(2)], axis=1)
            sums = jnp.dot(left, right, preferred_element_type=F32)
            if factor is not None:
                sums = factor * sums
            for k in range(2):
                s1[s, k, spots[k]] = sums[:, k * CH:(k + 1) * CH].astype(BF16)
            pl.when(i > 0)(lambda: start(i - 1))
            return carry

        lax.fori_loop(0, N, step, 0)

    def own_first(s, k):
        r1[s, k, place[k]] = s1[s, k, place[k]]

    def reduce_second(s, k):
        arrived(r1.at[s, k, pl.ds(0, 7)], rs1_(s, k))
        own_first(s, k)
        ring = 1 - k
        sums = [jnp.zeros((B, CH), F32) for _ in range(2)]
        for p in range(N):
            piece = r1[s, k, p].astype(F32)
            mark = crecv[k, p, 0:1, :]
            sums[0] = sums[0] + piece * (1.0 - mark)
            sums[1] = sums[1] + piece * mark
        s2[s, k] = jnp.concatenate([total.reshape(8, 8, CH) for total in sums], axis=1).astype(BF16)
        spread(ring, rs2_(s, k), lambda p: s2.at[s, k, p], r2.at[s, k])

    def owned(s, k):
        me = place[1 - k]
        r2[s, k, me] = s2[s, k, me]
        arrived(r2.at[s, k, pl.ds(0, 7)], rs2_(s, k))
        total = r2[s, k, 0].astype(F32)
        for p in range(1, N):
            total = total + r2[s, k, p].astype(F32)
        return total[:8], total[8:]

    def gather_second(s, k, piece0, piece1):
        ring = 1 - k
        a2s[s, k] = jnp.concatenate([piece0, piece1], axis=0).astype(BF16)
        spread(ring, ag2_(s, k), lambda p: a2s.at[s, k], a2r.at[s, k])

    def gather_first(s, k):
        a2r[s, k, place[1 - k]] = a2s[s, k]
        arrived(a2r.at[s, k, pl.ds(0, 7)], ag2_(s, k))
        both = a2r[s, k].astype(F32)
        zero, one = both[:, :8].reshape(B, CH), both[:, 8:].reshape(B, CH)
        for p in range(N):
            mark = crecv[k, p, 0:1, :]
            a1s[s, k, p] = (zero * (1.0 - mark) + one * mark).astype(BF16)
        spread(k, ag1_(s, k), lambda p: a1s.at[s, k, p], a1r.at[s, k])

    def gathered(s):
        for k in range(2):
            a1r[s, k, place[k]] = a1s[s, k, place[k]]
            arrived(a1r.at[s, k, pl.ds(0, 7)], ag1_(s, k))
            for p in range(N):
                f = chunk_of(k, p)
                wt[:, f * CH:(f + 1) * CH] = a1r[s, k, p]

    def project(quarter):
        rows = slice(quarter * 256, (quarter + 1) * 256)
        return rows, lax.dot_general(wt[...], xbuf[rows, :], (((1,), (1,)), ((), ())), preferred_element_type=F32)

    def upward(rows):
        first = rows.start // TOK
        return jnp.concatenate([rrecv[first].astype(F32), rrecv[first + 1].astype(F32)], axis=1)

    reduce_first(0)
    for k in range(2):
        arrived(crecv.at[k, pl.ds(0, 7)], C_ + k)
    for quarter in range(4):
        rows = slice(quarter * 256, (quarter + 1) * 256)
        curv[:, rows] = forget * upward(rows) * second_slope(prim[:, rows])
    for k in range(2):
        reduce_second(0, k)
    for k in range(2):
        grad0, grad1 = owned(0, k)
        base = wown[k, place[1 - k]]
        gather_second(0, k, base - rate0 * grad0, base - rate1 * grad1)
    for k in range(2):
        gather_first(0, k)
    gathered(0)

    for quarter in range(4):
        rows, value = project(quarter)
        delta[:, rows] = ((1.0 - 2.0 * forget) * upward(rows) * first_slope(value) / LEN).astype(BF16)
    reduce_first(1)
    for k in range(2):
        reduce_second(1, k)
    for k in range(2):
        outer0, outer1 = owned(1, k)
        osum[k] = outer0 + outer1
        gather_second(1, k, outer0, outer1)
    for k in range(2):
        gather_first(1, k)
    gathered(1)

    for quarter in range(4):
        rows, value = project(quarter)
        delta[:, rows] = (curv[:, rows] * value / LEN).astype(BF16)
    reduce_first(2, own_rate)
    for k in range(2):
        arrived(r1.at[2, k, pl.ds(0, 7)], rs1_(2, k))
        own_first(2, k)
        total = r1[2, k, 0].astype(F32)
        for p in range(1, N):
            total = total + r1[2, k, p].astype(F32)
        s2c[k] = total.reshape(8, 8, CH)
        spread(1 - k, rs2_(2, k), lambda p: s2c.at[k, p], r2c.at[k])
    for k in range(2):
        me = place[1 - k]
        r2c[k, me] = s2c[k, me]
        arrived(r2c.at[k, pl.ds(0, 7)], rs2_(2, k))
        total = r2c[k, 0]
        for p in range(1, N):
            total = total + r2c[k, p]
        tile[k] = SCALE * (osum[k] - total)

    spots = (yl, z % 4)
    targets = [spots[k] * 4 + yh * 2 + k for k in range(2)]
    for k in range(2):

        @pl.when(fs != targets[k])
        def _(k=k):
            send(tile.at[k], f1r.at[block], F1_ + k, F1_, (dp, targets[k]))

        @pl.when(fs == targets[k])
        def _(k=k):
            f1r[block] = tile[k]

    @pl.when(c == 0)
    def _():
        @pl.when(x == yl)
        def _():
            arrived(f1r.at[pl.ds(0, 7)], F1_)
            f2s[...] = f1r[...].reshape(4, 16, CH).astype(BF16)
            for o in range(1, NYL):
                send(f2s, f2r.at[0], F2_, F2_, (((yl + o) % NYL) * 8 + z, fs))
            f2r[0] = f2s[...]
            gone(f3r.at[pl.ds(0, 3)], F2_)

        @pl.when(x != yl)
        def _():
            arrived(f2r.at[0], F2_)

        def step(o, carry):
            p = (z + far_first(o)) % N
            send(f2r.at[0], f3r.at[z], F3_, F3_, ring_device(1, p))
            return carry

        lax.fori_loop(0, N - 1, step, 0)
        f3r[z] = f2r[0]

    @pl.when(c == 1)
    def _():
        @pl.when(x == z % 4)
        def _():
            arrived(f1r.at[pl.ds(0, 7)], F1_)
            f2s[...] = f1r[...].reshape(4, 16, CH).astype(BF16)

            def step(o, carry):
                p = (z + far_first(o)) % N
                send(f2s, f2r.at[z // 4], F2_, F2_ + z // 4, ring_device(1, p))
                return carry

            lax.fori_loop(0, N - 1, step, 0)
            f2r[z // 4] = f2s[...]
            arrived(f2r.at[1 - z // 4], F2_ + 1 - z // 4)
            gone(f3r.at[pl.ds(0, 7)], F2_)

        @pl.when(x != z % 4)
        def _():
            arrived(f2r.at[0], F2_)
            arrived(f2r.at[1], F2_ + 1)

        def step(o, carry):
            p = (y + far_first(o)) % N
            send(f2r.at[p // 4], f3r.at[y], F3_, F3_, ring_device(0, p))
            return carry

        lax.fori_loop(0, N - 1, step, 0)
        f3r[y] = f2r[yh]

    arrived(f3r.at[pl.ds(0, 7)], F3_)
    result = f3r[...].astype(F32).reshape(8, 8, 8, CH)
    for pair in range(4):
        both = jnp.concatenate([result[:, 2 * pair + i].reshape(B, CH) for i in range(2)], axis=0)
        out_ref[:, pair * 128:(pair + 1) * 128] = both.T

    gone(wx.at[pl.ds(0, 7)], W_)
    gone(wy.at[pl.ds(0, 7)], WY_)
    gone(rrecv.at[pl.ds(0, 7)], R_)
    gone(xbuf.at[pl.ds(0, 28 * QR)], X_)
    for k in range(2):
        gone(crecv.at[k, pl.ds(0, 7)], C_ + k)
        for s in range(3):
            gone(r1.at[s, k, pl.ds(0, 7)], rs1_(s, k))
        for s in range(2):
            gone(r2.at[s, k, pl.ds(0, 7)], rs2_(s, k))
            gone(a2r.at[s, k, pl.ds(0, 7)], ag2_(s, k))
            gone(a1r.at[s, k, pl.ds(0, 7)], ag1_(s, k))
        gone(r2c.at[k, pl.ds(0, 7)], rs2_(2, k))

        @pl.when(fs != targets[k])
        def _(k=k):
            gone(tile.at[k], F1_ + k)

    gone(f3r.at[pl.ds(0, 7)], F3_)


def local(tokens, upstream, value_weight, forget_label, copy_index, adv_rate):
    vmem, smem = pl.BlockSpec(memory_space=pltpu.VMEM), pl.BlockSpec(memory_space=pltpu.SMEM)
    hbm = pl.BlockSpec(memory_space=pl.ANY)
    return pl.pallas_call(
        kernel,
        out_shape=jax.ShapeDtypeStruct((CH, E), F32),
        in_specs=[hbm, hbm, hbm, smem, smem, smem],
        out_specs=vmem,
        scratch_shapes=[
            pltpu.VMEM((8 * TOK, DW), BF16),
            pltpu.VMEM((CH, E), BF16),
            pltpu.VMEM((TOK, E), BF16),
            pltpu.VMEM((8, 4, 16, CH), BF16),
            pltpu.VMEM((8, 16, CH), BF16),
            pltpu.VMEM((8, 8, 16, CH), BF16),
            pltpu.VMEM((8, B, TOK), BF16),
            pltpu.VMEM((8, B, TOK), BF16),
            pltpu.VMEM((2, 8, 8, 128), F32),
            pltpu.VMEM((B, DW), BF16),
            pltpu.VMEM((2, 8, 8, CH), F32),
            pltpu.VMEM((B, 8 * TOK), F32),
            pltpu.VMEM((B, 8 * TOK), F32),
            pltpu.VMEM((B, 8 * TOK), BF16),
            pltpu.VMEM((3, 2, 8, B, CH), BF16),
            pltpu.VMEM((3, 2, 8, B, CH), BF16),
            pltpu.VMEM((2, 2, 8, 16, CH), BF16),
            pltpu.VMEM((2, 2, 8, 16, CH), BF16),
            pltpu.VMEM((2, 8, 8, CH), F32),
            pltpu.VMEM((2, 8, 8, CH), F32),
            pltpu.VMEM((2, 2, 16, CH), BF16),
            pltpu.VMEM((2, 2, 8, 16, CH), BF16),
            pltpu.VMEM((2, 2, 8, B, CH), BF16),
            pltpu.VMEM((2, 2, 8, B, CH), BF16),
            pltpu.VMEM((2, 8, CH), F32),
            pltpu.VMEM((2, 8, CH), F32),
            pltpu.VMEM((8, 8, CH), F32),
            pltpu.VMEM((4, 16, CH), BF16),
            pltpu.VMEM((2, 4, 16, CH), BF16),
            pltpu.VMEM((8, 4, 16, CH), BF16),
            pltpu.SemaphoreType.DMA((GROUPS,)),
            pltpu.SemaphoreType.DMA((GROUPS,)),
            pltpu.SemaphoreType.DMA((3,)),
        ],
        compiler_params=pltpu.CompilerParams(collective_id=0, has_side_effects=True, vmem_limit_bytes=(64 << 20) - (400 << 10)),
        name="meta_grad",
    )(tokens, upstream, value_weight, forget_label, copy_index, adv_rate)


def solution(mesh):
    in_specs = (
        P(("dp", "fsdp"), None),
        P(("dp", "fsdp"), None),
        P("fsdp", None),
        P("dp"),
        P("dp"),
        P(),
    )
    return jax.shard_map(local, mesh=mesh, in_specs=in_specs, out_specs=P("fsdp", None), check_vma=False)
```

```python
import jax
import jax.numpy as jnp
from jax import lax
from jax.experimental import pallas as pl
from jax.experimental.pallas import tpu as pltpu
from jax.sharding import PartitionSpec as P

F32, BF16 = jnp.float32, jnp.bfloat16
NX, NYL, N = 4, 4, 8
TOK, DW, E, B, CH = 128, 2048, 512, 64, 128
LEN = 2048.0
SCALE = 8.0


def first_slope(value):
    sig = jax.nn.sigmoid(value)
    return sig * (1.0 + value * (1.0 - sig))


def second_slope(value):
    sig = jax.nn.sigmoid(value)
    return sig * (1.0 - sig) * (2.0 + value * (1.0 - 2.0 * sig))


QR = TOK // 4
W_, R_, C_ = 0, 1, 2


def rs1_(s, k):
    return 4 + 2 * s + k


def rs2_(s, k):
    return 10 + 2 * s + k


def ag2_(s, k):
    return 16 + 2 * s + k


def ag1_(s, k):
    return 20 + 2 * s + k


F1_, F2_, F3_, WY_, X_, GROUPS = 24, 26, 28, 29, 30, 63


def far_first(i):
    return 4 + (2 * (i % 2) - 1) * ((i + 1) // 2)


def chunk_of(k, p):
    return (p % 4) * 4 + (p // 4) * 2 + k


def kernel(
    tok_ref, up_ref, w_ref, forget_ref, copy_ref, rate_ref, out_ref,
    xbuf, wbuf, ubuf, wsrc, wx, wy, rsrc, rrecv, crecv, wt, wown, prim, curv, delta,
    s1, r1, s2, r2, s2c, r2c, a2s, a2r, a1s, a1r, osum, tile, f1r, f2s, f2r, f3r,
    ssem, rsem, lsem,
):
    dp, fs = lax.axis_index("dp"), lax.axis_index("fsdp")
    yl, z = dp // 8, dp % 8
    x, yh, c = fs // 4, (fs // 2) % 2, fs % 2
    y = yh * 4 + yl
    place = (y, z)

    def ring_device(ring, p):
        if ring == 0:
            return ((p % 4) * 8 + z, x * 4 + (p // 4) * 2 + c)
        return (yl * 8 + p, fs)

    def group_device(dx, dc):
        return (dp, ((x + dx) % NX) * 4 + yh * 2 + (c + dc) % 2)

    def send(src, dst, out_group, in_group, device):
        pltpu.make_async_remote_copy(
            src_ref=src, dst_ref=dst, send_sem=ssem.at[out_group], recv_sem=rsem.at[in_group],
            device_id=device, device_id_type=pl.DeviceIdType.MESH,
        ).start()

    def arrived(ref, group):
        pltpu.make_async_copy(ref, ref, rsem.at[group]).wait()

    def gone(ref, group):
        pltpu.make_async_copy(ref, ref, ssem.at[group]).wait()

    def spread(ring, group, source, dst):
        me = place[ring]

        def step(i, carry):
            p = (me + far_first(i)) % N
            send(source(p), dst.at[me], group, group, ring_device(ring, p))
            return carry

        lax.fori_loop(0, N - 1, step, 0)

    own = [
        pltpu.make_async_copy(src, dst, lsem.at[i])
        for i, (src, dst) in enumerate(((w_ref, wbuf), (up_ref, ubuf), (tok_ref, xbuf.at[pl.ds(0, TOK)])))
    ]
    for copy_in in own:
        copy_in.start()
    barrier = pltpu.get_barrier_semaphore()
    for dx in range(NX):
        for dc in range(2):
            if dx or dc:
                pl.semaphore_signal(barrier, inc=1, device_id=group_device(dx, dc), device_id_type=pl.DeviceIdType.MESH)
    for ring in range(2):

        def greet(o, carry, ring=ring):
            device = ring_device(ring, (place[ring] + o) % N)
            pl.semaphore_signal(barrier, inc=1, device_id=device, device_id_type=pl.DeviceIdType.MESH)
            return carry

        lax.fori_loop(1, N, greet, 0)

    own[0].wait()
    wsrc[...] = wbuf[...].T.reshape(8, 4, 16, CH)
    own[1].wait()
    rsrc[...] = ubuf[...].T.reshape(8, B, TOK)
    copy = copy_ref[0].astype(F32)
    forget = forget_ref[0].astype(F32)
    rate0, rate1 = rate_ref[0], rate_ref[1]
    own_rate = rate0 * (1.0 - copy) + rate1 * copy
    crecv[0, y] = jnp.full((8, 128), copy, F32)
    crecv[1, z] = jnp.full((8, 128), copy, F32)
    own[2].wait()
    pl.semaphore_wait(barrier, 21)

    block = 2 * x + c
    others = [(dx, dc) for dx in range(NX) for dc in range(2) if dx or dc]
    for dx, dc in others:
        to = 2 * ((x + dx) % NX) + (c + dc) % 2
        send(wsrc.at[to, yl], wx.at[block], W_, W_, group_device(dx, dc))

    def part(slot, quarter):
        return xbuf.at[pl.ds(slot * TOK + quarter * QR, QR)]

    def send_part(from_slot, to_slot, quarter, dx, dc):
        group = X_ + 1 + 4 * to_slot + quarter
        send(part(from_slot, quarter), part(to_slot, quarter), X_, group, group_device(dx, dc))

    def part_arrived(slot, quarter):
        arrived(part(slot, quarter), X_ + 1 + 4 * slot + quarter)

    for i in range(4):
        send_part(0, 6, i, 1, 0)
        send_part(0, 2, 3 - i, 3, 0)
        send_part(0, 1, i, 0, 1)
    for dx, dc in others:
        to = 2 * ((x + dx) % NX) + (c + dc) % 2
        send(rsrc.at[to], rrecv.at[2 * (-dx % NX) + dc], R_, R_, group_device(dx, dc))
    rrecv[0] = rsrc[block]
    for ring in range(2):
        spread(ring, C_ + ring, lambda p, ring=ring: crecv.at[ring, place[ring]], crecv.at[ring])

    wx[block] = wsrc[block, yl]
    arrived(wx.at[pl.ds(0, 7)], W_)
    spread(0, WY_, lambda p: wx, wy)
    wy[y] = wx[...]

    def first_pass(slot):
        rows = slice(slot * TOK, (slot + 1) * TOK)
        value = lax.dot_general(wt[...], xbuf[rows, :], (((1,), (1,)), ((), ())), preferred_element_type=F32)
        prim[:, rows] = value
        delta[:, rows] = (forget * rrecv[slot].astype(F32) * first_slope(value) / LEN).astype(BF16)

    def pass_on(slot, quarter):
        part_arrived(slot, quarter)
        send_part(slot, slot + 1, quarter, 0, 1)

    for i in range(2):
        part_arrived(6, i)
        send_part(6, 4, i, 1, 0)
        send_part(6, 7, i, 0, 1)
        part_arrived(2, 3 - i)
        send_part(2, 4, 3 - i, 3, 0)
        send_part(2, 3, 3 - i, 0, 1)
    for i in range(2):
        pass_on(6, 2 + i)
        pass_on(2, 1 - i)
    arrived(wy.at[pl.ds(0, 7)], WY_)
    for p in range(N):
        for b in range(8):
            f = (b // 2) * 4 + (p // 4) * 2 + b % 2
            wt[(p % 4) * 16:(p % 4) * 16 + 16, f * CH:(f + 1) * CH] = wy[p, b]
    for k in range(2):
        first = pl.multiple_of(chunk_of(k, place[k]) * CH, CH)
        wown[k] = wt[:, pl.ds(first, CH)].astype(F32).reshape(8, 8, CH)
    for i in range(4):
        part_arrived(1, i)
    arrived(rrecv.at[pl.ds(0, 7)], R_)
    first_pass(0)
    first_pass(1)
    pass_on(4, 0)
    pass_on(4, 3)
    first_pass(6)
    first_pass(2)
    for slot in (7, 3):
        for i in range(4):
            part_arrived(slot, i)
        first_pass(slot)
    pass_on(4, 1)
    pass_on(4, 2)
    first_pass(4)
    for i in range(4):
        part_arrived(5, i)
    first_pass(5)

    def reduce_first(s, factor=None):
        left = delta[...]
        for quarter in range(4):
            sums = jnp.dot(left, xbuf[:, quarter * 512:(quarter + 1) * 512], preferred_element_type=F32)
            if factor is not None:
                sums = factor * sums
            for i in range(4):
                f = 4 * quarter + i
                s1[s, f % 2, f // 4 + 4 * ((f // 2) % 2)] = sums[:, i * CH:(i + 1) * CH].astype(BF16)

        def start(i, carry):
            for k in range(2):
                p = (place[k] + far_first(i)) % N
                send(s1.at[s, k, p], r1.at[s, k, place[k]], rs1_(s, k), rs1_(s, k), ring_device(k, p))
            return carry

        lax.fori_loop(0, N - 1, start, 0)

    def own_first(s, k):
        r1[s, k, place[k]] = s1[s, k, place[k]]

    def reduce_second(s, k):
        arrived(r1.at[s, k, pl.ds(0, 7)], rs1_(s, k))
        own_first(s, k)
        ring = 1 - k
        sums = [jnp.zeros((B, CH), F32) for _ in range(2)]
        for p in range(N):
            piece = r1[s, k, p].astype(F32)
            mark = crecv[k, p, 0:1, :]
            sums[0] = sums[0] + piece * (1.0 - mark)
            sums[1] = sums[1] + piece * mark
        s2[s, k] = jnp.concatenate([total.reshape(8, 8, CH) for total in sums], axis=1).astype(BF16)
        spread(ring, rs2_(s, k), lambda p: s2.at[s, k, p], r2.at[s, k])

    def owned(s, k):
        me = place[1 - k]
        r2[s, k, me] = s2[s, k, me]
        arrived(r2.at[s, k, pl.ds(0, 7)], rs2_(s, k))
        total = r2[s, k, 0].astype(F32)
        for p in range(1, N):
            total = total + r2[s, k, p].astype(F32)
        return total[:8], total[8:]

    def gather_second(s, k, piece0, piece1):
        ring = 1 - k
        a2s[s, k] = jnp.concatenate([piece0, piece1], axis=0).astype(BF16)
        spread(ring, ag2_(s, k), lambda p: a2s.at[s, k], a2r.at[s, k])

    def gather_first(s, k):
        a2r[s, k, place[1 - k]] = a2s[s, k]
        arrived(a2r.at[s, k, pl.ds(0, 7)], ag2_(s, k))
        both = a2r[s, k].astype(F32)
        zero, one = both[:, :8].reshape(B, CH), both[:, 8:].reshape(B, CH)
        for p in range(N):
            mark = crecv[k, p, 0:1, :]
            a1s[s, k, p] = (zero * (1.0 - mark) + one * mark).astype(BF16)
        spread(k, ag1_(s, k), lambda p: a1s.at[s, k, p], a1r.at[s, k])

    def gathered(s):
        for k in range(2):
            a1r[s, k, place[k]] = a1s[s, k, place[k]]
            arrived(a1r.at[s, k, pl.ds(0, 7)], ag1_(s, k))
            for p in range(N):
                f = chunk_of(k, p)
                wt[:, f * CH:(f + 1) * CH] = a1r[s, k, p]

    def project(quarter):
        rows = slice(quarter * 256, (quarter + 1) * 256)
        return rows, lax.dot_general(wt[...], xbuf[rows, :], (((1,), (1,)), ((), ())), preferred_element_type=F32)

    def upward(rows):
        first = rows.start // TOK
        return jnp.concatenate([rrecv[first].astype(F32), rrecv[first + 1].astype(F32)], axis=1)

    reduce_first(0)
    for k in range(2):
        arrived(crecv.at[k, pl.ds(0, 7)], C_ + k)
    for quarter in range(4):
        rows = slice(quarter * 256, (quarter + 1) * 256)
        curv[:, rows] = forget * upward(rows) * second_slope(prim[:, rows])
    for k in range(2):
        reduce_second(0, k)
    for k in range(2):
        grad0, grad1 = owned(0, k)
        base = wown[k, place[1 - k]]
        gather_second(0, k, base - rate0 * grad0, base - rate1 * grad1)
    for k in range(2):
        gather_first(0, k)
    gathered(0)

    for quarter in range(4):
        rows, value = project(quarter)
        delta[:, rows] = ((1.0 - 2.0 * forget) * upward(rows) * first_slope(value) / LEN).astype(BF16)
    reduce_first(1)
    for k in range(2):
        reduce_second(1, k)
    for k in range(2):
        outer0, outer1 = owned(1, k)
        osum[k] = outer0 + outer1
        gather_second(1, k, outer0, outer1)
    for k in range(2):
        gather_first(1, k)
    gathered(1)

    for quarter in range(4):
        rows, value = project(quarter)
        delta[:, rows] = (curv[:, rows] * value / LEN).astype(BF16)
    reduce_first(2, own_rate)
    for k in range(2):
        arrived(r1.at[2, k, pl.ds(0, 7)], rs1_(2, k))
        own_first(2, k)
        total = r1[2, k, 0].astype(F32)
        for p in range(1, N):
            total = total + r1[2, k, p].astype(F32)
        s2c[k] = total.reshape(8, 8, CH)
        spread(1 - k, rs2_(2, k), lambda p: s2c.at[k, p], r2c.at[k])
    for k in range(2):
        me = place[1 - k]
        r2c[k, me] = s2c[k, me]
        arrived(r2c.at[k, pl.ds(0, 7)], rs2_(2, k))
        total = r2c[k, 0]
        for p in range(1, N):
            total = total + r2c[k, p]
        tile[k] = SCALE * (osum[k] - total)

    spots = (yl, z % 4)
    targets = [spots[k] * 4 + yh * 2 + k for k in range(2)]
    for k in range(2):

        @pl.when(fs != targets[k])
        def _(k=k):
            send(tile.at[k], f1r.at[block], F1_ + k, F1_, (dp, targets[k]))

        @pl.when(fs == targets[k])
        def _(k=k):
            f1r[block] = tile[k]

    @pl.when(c == 0)
    def _():
        @pl.when(x == yl)
        def _():
            arrived(f1r.at[pl.ds(0, 7)], F1_)
            f2s[...] = f1r[...].reshape(4, 16, CH).astype(BF16)
            for o in range(1, NYL):
                send(f2s, f2r.at[0], F2_, F2_, (((yl + o) % NYL) * 8 + z, fs))
            f2r[0] = f2s[...]
            gone(f3r.at[pl.ds(0, 3)], F2_)

        @pl.when(x != yl)
        def _():
            arrived(f2r.at[0], F2_)

        def step(o, carry):
            p = (z + far_first(o)) % N
            send(f2r.at[0], f3r.at[z], F3_, F3_, ring_device(1, p))
            return carry

        lax.fori_loop(0, N - 1, step, 0)
        f3r[z] = f2r[0]

    @pl.when(c == 1)
    def _():
        @pl.when(x == z % 4)
        def _():
            arrived(f1r.at[pl.ds(0, 7)], F1_)
            f2s[...] = f1r[...].reshape(4, 16, CH).astype(BF16)

            def step(o, carry):
                p = (z + far_first(o)) % N
                send(f2s, f2r.at[z // 4], F2_, F2_ + z // 4, ring_device(1, p))
                return carry

            lax.fori_loop(0, N - 1, step, 0)
            f2r[z // 4] = f2s[...]
            arrived(f2r.at[1 - z // 4], F2_ + 1 - z // 4)
            gone(f3r.at[pl.ds(0, 7)], F2_)

        @pl.when(x != z % 4)
        def _():
            arrived(f2r.at[0], F2_)
            arrived(f2r.at[1], F2_ + 1)

        def step(o, carry):
            p = (y + far_first(o)) % N
            send(f2r.at[p // 4], f3r.at[y], F3_, F3_, ring_device(0, p))
            return carry

        lax.fori_loop(0, N - 1, step, 0)
        f3r[y] = f2r[yh]

    arrived(f3r.at[pl.ds(0, 7)], F3_)
    result = f3r[...].astype(F32).reshape(8, 8, 8, CH)
    for pair in range(4):
        both = jnp.concatenate([result[:, 2 * pair + i].reshape(B, CH) for i in range(2)], axis=0)
        out_ref[:, pair * 128:(pair + 1) * 128] = both.T

    gone(wx.at[pl.ds(0, 7)], W_)
    gone(wy.at[pl.ds(0, 7)], WY_)
    gone(rrecv.at[pl.ds(0, 7)], R_)
    gone(xbuf.at[pl.ds(0, 28 * QR)], X_)
    for k in range(2):
        gone(crecv.at[k, pl.ds(0, 7)], C_ + k)
        for s in range(3):
            gone(r1.at[s, k, pl.ds(0, 7)], rs1_(s, k))
        for s in range(2):
            gone(r2.at[s, k, pl.ds(0, 7)], rs2_(s, k))
            gone(a2r.at[s, k, pl.ds(0, 7)], ag2_(s, k))
            gone(a1r.at[s, k, pl.ds(0, 7)], ag1_(s, k))
        gone(r2c.at[k, pl.ds(0, 7)], rs2_(2, k))

        @pl.when(fs != targets[k])
        def _(k=k):
            gone(tile.at[k], F1_ + k)

    gone(f3r.at[pl.ds(0, 7)], F3_)


def local(tokens, upstream, value_weight, forget_label, copy_index, adv_rate):
    vmem, smem = pl.BlockSpec(memory_space=pltpu.VMEM), pl.BlockSpec(memory_space=pltpu.SMEM)
    hbm = pl.BlockSpec(memory_space=pl.ANY)
    return pl.pallas_call(
        kernel,
        out_shape=jax.ShapeDtypeStruct((CH, E), F32),
        in_specs=[hbm, hbm, hbm, smem, smem, smem],
        out_specs=vmem,
        scratch_shapes=[
            pltpu.VMEM((8 * TOK, DW), BF16),
            pltpu.VMEM((CH, E), BF16),
            pltpu.VMEM((TOK, E), BF16),
            pltpu.VMEM((8, 4, 16, CH), BF16),
            pltpu.VMEM((8, 16, CH), BF16),
            pltpu.VMEM((8, 8, 16, CH), BF16),
            pltpu.VMEM((8, B, TOK), BF16),
            pltpu.VMEM((8, B, TOK), BF16),
            pltpu.VMEM((2, 8, 8, 128), F32),
            pltpu.VMEM((B, DW), BF16),
            pltpu.VMEM((2, 8, 8, CH), F32),
            pltpu.VMEM((B, 8 * TOK), F32),
            pltpu.VMEM((B, 8 * TOK), F32),
            pltpu.VMEM((B, 8 * TOK), BF16),
            pltpu.VMEM((3, 2, 8, B, CH), BF16),
            pltpu.VMEM((3, 2, 8, B, CH), BF16),
            pltpu.VMEM((2, 2, 8, 16, CH), BF16),
            pltpu.VMEM((2, 2, 8, 16, CH), BF16),
            pltpu.VMEM((2, 8, 8, CH), F32),
            pltpu.VMEM((2, 8, 8, CH), F32),
            pltpu.VMEM((2, 2, 16, CH), BF16),
            pltpu.VMEM((2, 2, 8, 16, CH), BF16),
            pltpu.VMEM((2, 2, 8, B, CH), BF16),
            pltpu.VMEM((2, 2, 8, B, CH), BF16),
            pltpu.VMEM((2, 8, CH), F32),
            pltpu.VMEM((2, 8, CH), F32),
            pltpu.VMEM((8, 8, CH), F32),
            pltpu.VMEM((4, 16, CH), BF16),
            pltpu.VMEM((2, 4, 16, CH), BF16),
            pltpu.VMEM((8, 4, 16, CH), BF16),
            pltpu.SemaphoreType.DMA((GROUPS,)),
            pltpu.SemaphoreType.DMA((GROUPS,)),
            pltpu.SemaphoreType.DMA((3,)),
        ],
        compiler_params=pltpu.CompilerParams(collective_id=0, has_side_effects=True, vmem_limit_bytes=(64 << 20) - (400 << 10)),
        name="meta_grad",
    )(tokens, upstream, value_weight, forget_label, copy_index, adv_rate)


def solution(mesh):
    in_specs = (
        P(("dp", "fsdp"), None),
        P(("dp", "fsdp"), None),
        P("fsdp", None),
        P("dp"),
        P("dp"),
        P(),
    )
    return jax.shard_map(local, mesh=mesh, in_specs=in_specs, out_specs=P("fsdp", None), check_vma=False)
```
